32 devices in a mesh: cell: 8 (over z, y), grp: 4 (over x, core).
Axes of the slice: x: 2, y: 2, z: 4, core: 2. Of those that a mesh axis runs over, the one named last changes fastest.
Arguments:
- initial_guess: float32 [9, 6144], P(None, 'cell'), may hold values from -3 to 3
- right_side: float32 [9, 6144], P(None, 'cell')
- camera_blocks: float32 [9, 9, 6144], P(None, None, 'cell'), as said below
- point_inverse: float32 [3, 3, 16384], P(None, None, ('cell', 'grp')), as said below
- jacobian_tiles: bfloat16 [192, 576, 384], P(('cell', 'grp'))
- tile_pattern: int32 [192, 2], P(('cell', 'grp')), may hold values from 0 to 35, as said below
- cell_load: int32 [8], P('cell'), may hold values from 2 to 6, as said below
Outputs:
- solution: float32 [9, 6144], P(None, 'cell')
- residual: float32 [9, 6144], P(None, 'cell')
The draws below stay inside these ranges and needn't reach their ends.
Inputs may be any that keep to these rules, and one draw needn't show every extreme that they name: `tile_pattern`: column 0 is below 36, column 1 below 4. `cell_load`: A quarter of the cells, rounded down, chosen from the seed, have 6 live slots on each of their devices; every other cell has 2. Slots at or past the load are unused. `camera_blocks`: each camera block is symmetric with a dominant diagonal. `point_inverse`: each point's block is symmetric with a dominant diagonal.
All inputs are finite; a program needn't handle non-finite values.
Results may differ from the reference program's by a relative error of at most 0.0095.
Values may be sent and summed in bfloat16 or wider, within the bound.
A program may use at most 64 MiB of HBM per device.

```python
import math
from functools import partial
import jax
import jax.numpy as jnp
from jax import lax

CAM_PARAMS = 9
PT_PARAMS = 3
CAM_TILE = 64
PT_TILE = 128
CAM_TILES = 12
PT_TILES = 4
SLOTS = 6
ITERS = 2
CELLS = 8
GRPS = 4
CAMERAS = 6144
POINTS = 16384
TILES = 192


def draw_right_side(key, part):
    position = jnp.arange(CAMERAS, dtype=jnp.float32) / CAMERAS
    rising = jnp.exp(math.log(3.0) * position)[None, :]
    return jax.random.truncated_normal(key, -4.0, 4.0, (CAM_PARAMS, CAMERAS), jnp.float32) * rising


def symmetric_blocks(key, size, columns, offset, low, high):
    raw = jax.random.uniform(key, (size, size, columns), jnp.float32, -offset, offset)
    mirrored = 0.5 * (raw + raw.transpose(1, 0, 2))
    diagonal = jax.random.uniform(jax.random.fold_in(key, 7), (size, columns), jnp.float32, low, high)
    identity = (jnp.arange(size)[:, None] == jnp.arange(size)[None, :]).astype(jnp.float32)
    return mirrored * (1.0 - identity)[:, :, None] + identity[:, :, None] * diagonal[:, None, :]


def draw_camera_blocks(key, part):
    return symmetric_blocks(key, CAM_PARAMS, CAMERAS, 0.06, 1.5, 3.0)


def draw_point_inverse(key, part):
    return symmetric_blocks(key, PT_PARAMS, POINTS, 0.15, 0.5, 1.0)


def draw_jacobian_tiles(key, part):
    rows = CAM_PARAMS * CAM_TILE
    columns = PT_PARAMS * PT_TILE
    half = 0.3 * math.sqrt(3.0) / math.sqrt(rows + columns)
    base = jax.random.uniform(key, (TILES, rows, columns), jnp.float32, -half, half)
    return base.astype(jnp.bfloat16)


def draw_tile_pattern(key, part):
    window = jax.random.randint(key, (TILES, 1), 0, 3 * CAM_TILES, dtype=jnp.int32)
    points = jax.random.randint(jax.random.fold_in(key, 5), (TILES, 1), 0, PT_TILES, dtype=jnp.int32)
    return jnp.concatenate([window, points], axis=1)


def draw_cell_load(key, part):
    ranking = jax.random.permutation(key, CELLS)
    return jnp.where(ranking < CELLS // 4, SLOTS, SLOTS // 3).astype(jnp.int32)


def block_scale(key, shape, pieces, smallest, top_value):
    gain, own = 1.0, jax.random.fold_in(key, 6)
    for axis_at, parts in pieces:
        heights = jnp.exp(jax.random.uniform(jax.random.fold_in(own, axis_at), (parts,), jnp.float32, smallest / len(pieces), top_value / len(pieces)))
        gain = gain * jnp.repeat(heights, shape[axis_at] // parts).reshape([-1 if axis == axis_at else 1 for axis in range(len(shape))])
    return gain


def centred(key, shape, width, limit, split=(), kind=jnp.bfloat16):
    drawn = width * jax.random.normal(key, shape, jnp.float32)
    if split:
        drawn = drawn * block_scale(key, shape, split, -0.22, 0.18)
    return jnp.clip(drawn, -limit, limit).astype(kind)


def setup_inputs(seed: int = 0) -> dict:
    seeds = jax.random.split(jax.random.key(seed), 8)
    initial_guess = centred(seeds[0], (CAM_PARAMS, CAMERAS), 0.5, 3.0, ((1, 8),), jnp.float32)
    right_side = draw_right_side(jax.random.fold_in(seeds[7], 71), 0)
    camera_blocks = draw_camera_blocks(jax.random.fold_in(seeds[7], 71), 0)
    point_inverse = draw_point_inverse(jax.random.fold_in(seeds[7], 71), 0)
    jacobian_tiles = draw_jacobian_tiles(jax.random.fold_in(seeds[7], 71), 0)
    tile_pattern = draw_tile_pattern(jax.random.fold_in(seeds[7], 71), 0)
    cell_load = draw_cell_load(jax.random.fold_in(seeds[7], 71), 0)
    return dict(initial_guess=initial_guess, right_side=right_side, camera_blocks=camera_blocks, point_inverse=point_inverse, jacobian_tiles=jacobian_tiles, tile_pattern=tile_pattern, cell_load=cell_load)


HIGHEST = lax.Precision.HIGHEST


def tile_rows(camera_field, tile_width):
    components = camera_field.shape[0]
    return camera_field.reshape(components, -1, tile_width).transpose(1, 0, 2).reshape(-1, components * tile_width)


def schur_apply(direction, camera_blocks, point_inverse, jacobian_tiles, tile_pattern, cell_load):
    lowered = direction.astype(jnp.bfloat16)
    camera_rows = tile_rows(lowered, CAM_TILE)
    devices = CELLS * GRPS
    tiles_dev = jacobian_tiles.reshape(devices, SLOTS, CAM_PARAMS * CAM_TILE, PT_PARAMS * PT_TILE)
    pattern_dev = tile_pattern.reshape(devices, SLOTS, 2)
    inverse_dev = point_inverse.reshape(PT_PARAMS, PT_PARAMS, devices, PT_TILES, PT_TILE).transpose(2, 0, 1, 3, 4)

    def one_device(device_items):
        device, device_tiles, pattern, inverse = device_items
        cell_index = device // GRPS
        window = pattern[:, 0]
        cam_tile = ((cell_index - 1 + window // CAM_TILES) % CELLS) * CAM_TILES + window % CAM_TILES
        cam_tile = cam_tile.astype(jnp.int32)
        live_mask = (jnp.arange(SLOTS, dtype=jnp.int32) < cell_load[cell_index]).astype(jnp.float32)
        tiles_wide = device_tiles.astype(jnp.float32)
        chosen = camera_rows[cam_tile].astype(jnp.float32)
        forward = jnp.einsum("tk,tkj->tj", chosen, tiles_wide, precision=HIGHEST) * live_mask[:, None]
        point_sums = jax.ops.segment_sum(forward, pattern[:, 1], PT_TILES)
        solved = jnp.einsum("jipq,piq->pjq", inverse, point_sums.reshape(PT_TILES, PT_PARAMS, PT_TILE), precision=HIGHEST)
        solved = solved.reshape(PT_TILES, PT_PARAMS * PT_TILE).astype(jnp.bfloat16)
        gathered = solved[pattern[:, 1]].astype(jnp.float32)
        backward = jnp.einsum("tj,tkj->tk", gathered, tiles_wide, precision=HIGHEST) * live_mask[:, None]
        return backward, cam_tile

    backward, cam_tile = lax.map(one_device, (jnp.arange(devices, dtype=jnp.int32), tiles_dev, pattern_dev, inverse_dev))
    back_rows = jax.ops.segment_sum(backward.reshape(-1, CAM_PARAMS * CAM_TILE), cam_tile.reshape(-1), CELLS * CAM_TILES)
    back_field = back_rows.reshape(CELLS * CAM_TILES, CAM_PARAMS, CAM_TILE).transpose(1, 0, 2).reshape(CAM_PARAMS, -1)
    return jnp.einsum("klc,lc->kc", camera_blocks, direction, precision=HIGHEST) - back_field


def reference(initial_guess, right_side, camera_blocks, point_inverse, jacobian_tiles, tile_pattern, cell_load):
    operate = partial(schur_apply, camera_blocks=camera_blocks, point_inverse=point_inverse, jacobian_tiles=jacobian_tiles, tile_pattern=tile_pattern, cell_load=cell_load)
    diagonal_part = jnp.diagonal(camera_blocks, axis1=0, axis2=1).T
    solution = initial_guess
    residual = right_side - operate(solution)
    precond = residual / diagonal_part
    direction = precond
    rz_now = jnp.sum(residual * precond)
    for iteration in range(ITERS):
        image = operate(direction)
        step_size = rz_now / jnp.sum(direction * image)
        solution = solution + step_size * direction
        residual = residual - step_size * image
        precond = residual / diagonal_part
        rz_next = jnp.sum(residual * precond)
        direction = precond + (rz_next / rz_now) * direction
        rz_now = rz_next
    return solution, residual
```

```python
import functools

import jax
import jax.numpy as jnp
from jax import lax
from jax.experimental import pallas as pl
from jax.experimental.pallas import tpu as pltpu
from jax.sharding import PartitionSpec as P

CAM_TILE = 64
ITERS = 2
REACH = 2
SPAN = 2 * REACH + 1
LANES = 128
ROWS = 8
MESH = pl.DeviceIdType.MESH
F32 = jnp.float32
BF16 = jnp.bfloat16


def kernel(
    cells,
    grps,
    guess_hbm,
    right_hbm,
    blocks_hbm,
    inverse_hbm,
    jac_hbm,
    pattern,
    load,
    solution_ref,
    residual_ref,
    guess,
    right,
    blocks,
    inverse,
    jac,
    window,
    guess_send,
    guess_recv,
    halo_send,
    halo_recv,
    image_send,
    image_recv,
    pattern_send,
    pattern_recv,
    slot_send,
    slot_recv,
    scalar_send,
    scalar_recv,
    local_sem,
    jac_sem,
    halo_send_sem,
    halo_recv_sem,
    image_send_sem,
    image_recv_sem,
    pattern_sem,
    slot_send_sem,
    slot_recv_sem,
    scalar_sem,
):
    params, cameras = guess.shape
    slots, rows_wide, points_wide = jac.shape
    tiles = cameras // CAM_TILE
    pairs = cameras // LANES
    coords = inverse.shape[0]
    point_tiles = inverse.shape[2] // LANES
    devices = cells * grps
    cell = lax.axis_index("cell")
    grp = lax.axis_index("grp")
    me = cell * grps + grp

    local = [
        pltpu.make_async_copy(src, dst, local_sem.at[i])
        for i, (src, dst) in enumerate(
            ((guess_hbm, guess), (blocks_hbm, blocks), (right_hbm, right), (inverse_hbm, inverse))
        )
    ]
    jac_copies = [
        pltpu.make_async_copy(jac_hbm.at[s], jac.at[s], jac_sem.at[s]) for s in range(slots)
    ]
    for copy in local:
        copy.start()
    for copy in jac_copies:
        copy.start()

    barrier = pltpu.get_barrier_semaphore()

    def greet(i, carry):
        other = lax.rem(me + i, devices)
        pl.semaphore_signal(
            barrier, inc=1, device_id=(other // grps, lax.rem(other, grps)), device_id_type=MESH
        )
        return carry

    lax.fori_loop(1, devices, greet, 0)

    def near(delta, turn):
        return (lax.rem(cell + delta + cells, cells), lax.rem(grp + turn, grps))

    def slot_index(delta, turn):
        return (delta % SPAN) * grps + turn % grps

    def peers(reach):
        found = []
        for delta in sorted(range(-reach, reach + 1), key=lambda d: -abs(d)):
            for turn in range(grps):
                if delta != 0 or turn != 0:
                    found.append((delta, turn))
        return found

    def iota(shape, axis):
        return lax.broadcasted_iota(jnp.int32, shape, axis)

    lane8 = iota((ROWS, LANES), 1)
    row8 = iota((ROWS, LANES), 0)
    lane9 = iota((params, LANES), 1)
    row9 = iota((params, LANES), 0)
    low9 = lane9 < CAM_TILE
    chunks = (rows_wide + LANES - 1) // LANES
    own_rows = [row9 == 2 * b + (lane9 >= CAM_TILE).astype(jnp.int32) for b in range(chunks)]

    live = [s < load[0] for s in range(slots)]
    ids = [pattern[s, 0] for s in range(slots)]
    point_ids = [pattern[s, 1] for s in range(slots)]
    id_rows = jnp.full((ROWS, LANES), -4096, jnp.int32)
    point_rows = jnp.full((ROWS, LANES), -1, jnp.int32)
    for s in range(slots):
        id_rows = jnp.where(row8 == s, jnp.where(live[s], ids[s], -4096), id_rows)
        point_rows = jnp.where(row8 == s, point_ids[s], point_rows)
    pattern_send[...] = id_rows
    pattern_recv[0] = id_rows

    def pack(field):
        tail = jnp.zeros((ROWS, LANES), F32)
        for i in range(pairs):
            tail = jnp.where(row8 == i, field[ROWS:, i * LANES : (i + 1) * LANES], tail)
        return jnp.concatenate([field[:ROWS], tail], axis=1)

    def unpack(packed):
        return [
            jnp.concatenate(
                [packed[:, i * LANES : (i + 1) * LANES], packed[i : i + 1, cameras:]], axis=0
            )
            for i in range(pairs)
        ]

    def blocks_of(field):
        return [field[:, i * LANES : (i + 1) * LANES] for i in range(pairs)]

    local[0].wait()
    guess_send[...] = pack(guess[...]).astype(BF16)
    local[1].wait()

    def block_product(field):
        total = blocks[0] * field[0:1, :]
        for k in range(1, params):
            total = total + blocks[k] * field[k : k + 1, :]
        return total

    row_wide = iota((params, cameras), 0)
    diagonal = blocks[0]
    for k in range(1, params):
        diagonal = jnp.where(row_wide == k, blocks[k], diagonal)
    scale = 1.0 / diagonal
    local[2].wait()
    residual0 = right[...] - block_product(guess[...])
    halo_send[0] = pack(residual0 * scale)
    halo_send[1] = pack(scale)
    local[3].wait()
    inverse_rows = []
    for j in range(coords):
        for i in range(coords):
            picked = jnp.zeros((ROWS, LANES), F32)
            for q in range(point_tiles):
                picked = jnp.where(
                    point_rows == q, inverse[j, i : i + 1, q * LANES : (q + 1) * LANES], picked
                )
            inverse_rows.append(picked)
    pad = jnp.zeros((ROWS, chunks * LANES - rows_wide), F32)

    pl.semaphore_wait(barrier, devices - 1)

    halo_copies = []
    for part in range(3):
        for side, delta in ((0, 1), (1, -1)):
            copy = pltpu.make_async_remote_copy(
                src_ref=guess_send if part == 0 else halo_send.at[part - 1],
                dst_ref=guess_recv.at[side] if part == 0 else halo_recv.at[side, part - 1],
                send_sem=halo_send_sem.at[side, part],
                recv_sem=halo_recv_sem.at[side, part],
                device_id=near(delta, 0),
                device_id_type=MESH,
            )
            halo_copies.append(copy)
    halo_copies[0].start()
    halo_copies[1].start()
    for delta, turn in peers(REACH):
        pltpu.make_async_remote_copy(
            src_ref=pattern_send,
            dst_ref=pattern_recv.at[slot_index(-delta, -turn)],
            send_sem=pattern_sem.at[0],
            recv_sem=pattern_sem.at[1],
            device_id=near(delta, turn),
            device_id_type=MESH,
        ).start()
    for copy in halo_copies[2:]:
        copy.start()

    def put(side, parts):
        for i in range(pairs):
            window[side * pairs + i] = parts[i]

    def slot_rows():
        forward = jnp.zeros((ROWS, points_wide), F32)
        row_points = iota((ROWS, points_wide), 0)
        for s in range(slots):
            block = window[lax.shift_right_logical(ids[s], 1)]
            turned = pltpu.roll(block, CAM_TILE, 1)
            odd = lax.bitwise_and(ids[s], 1)
            keep = jnp.where(low9, 0, 1) == odd
            tile = jnp.where(keep, block, turned)
            tile = jnp.where(live[s], tile, 0.0)
            spread = jnp.concatenate([jnp.where(own, tile, 0.0) for own in own_rows], axis=1)
            left = spread[:, :rows_wide].astype(BF16)
            product = jnp.dot(left, jac[s], preferred_element_type=F32)
            total = jnp.sum(product, axis=0, keepdims=True)
            forward = jnp.where(row_points == s, total, forward)
        wide_points = jnp.concatenate([point_rows] * coords, axis=1)
        sums = jnp.zeros((ROWS, points_wide), F32)
        for s in range(slots):
            sums = sums + jnp.where(wide_points == point_ids[s], forward[s : s + 1, :], 0.0)
        solved = []
        for j in range(coords):
            total = inverse_rows[j * coords] * sums[:, :LANES]
            for i in range(1, coords):
                total = total + inverse_rows[j * coords + i] * sums[:, i * LANES : (i + 1) * LANES]
            solved.append(total)
        solved = jnp.concatenate(solved, axis=1).astype(BF16)
        energy = forward * solved.astype(F32)
        backward = jnp.zeros((ROWS, rows_wide), F32)
        row_cams = iota((ROWS, rows_wide), 0)
        for s in range(slots):
            product = lax.dot_general(
                solved, jac[s], (((1,), (1,)), ((), ())), preferred_element_type=F32
            )
            backward = jnp.where(row_cams == s, jnp.where(live[s], product, 0.0), backward)
        backward = jnp.concatenate([backward, pad], axis=1).astype(BF16)
        energy_lanes = energy[:, :LANES]
        for i in range(1, coords):
            energy_lanes = energy_lanes + energy[:, i * LANES : (i + 1) * LANES]
        return backward, jnp.sum(energy_lanes, axis=0, keepdims=True)

    def send_slots(turn_no, backward):
        slot_send[turn_no] = backward
        slot_recv[turn_no, 0] = backward
        for delta, turn in peers(REACH):
            pltpu.make_async_remote_copy(
                src_ref=slot_send.at[turn_no],
                dst_ref=slot_recv.at[turn_no, slot_index(-delta, -turn)],
                send_sem=slot_send_sem.at[turn_no],
                recv_sem=slot_recv_sem.at[turn_no],
                device_id=near(delta, turn),
                device_id_type=MESH,
            ).start()

    others = pl.ds(1, SPAN * grps - 1)

    def wait_bytes(ref, sem):
        pltpu.make_async_copy(ref, ref, sem).wait()

    def gather_back(turn_no, chooser, sides):
        wait_bytes(slot_recv.at[turn_no, others], slot_recv_sem.at[turn_no])
        stacked = slot_recv[turn_no].astype(F32).reshape(SPAN * grps * ROWS, chunks * LANES)
        summed = jnp.dot(chooser, stacked.astype(BF16), preferred_element_type=F32)
        fields = []
        for side in sides:
            parts = []
            for i in range(pairs):
                first = side * tiles + 2 * i
                both = []
                for t in (first, first + 1):
                    total = jnp.zeros((params, LANES), F32)
                    for b in range(chunks):
                        piece = summed[t : t + 1, b * LANES : (b + 1) * LANES]
                        total = jnp.where(own_rows[b], piece, total)
                    both.append(total)
                parts.append(
                    jnp.where(low9, both[0], both[1])
                    + pltpu.roll(jnp.where(low9, both[1], both[0]), CAM_TILE, 1)
                )
            fields.append(parts)
        return fields

    put(1, blocks_of(guess[...]))
    halo_copies[0].wait()
    halo_copies[1].wait()
    put(0, unpack(guess_recv[0].astype(F32)))
    put(2, unpack(guess_recv[1].astype(F32)))
    for copy in jac_copies:
        copy.wait()
    backward, _ = slot_rows()
    send_slots(0, backward)

    wait_bytes(pattern_recv.at[others], pattern_sem.at[1])
    columns = []
    for shift in range(SPAN):
        delta = shift if shift <= REACH else shift - SPAN
        for turn in range(grps):
            at = pattern_recv[shift * grps + turn] + delta * tiles
            columns.append((at == lane8).astype(F32))
    chosen = jnp.concatenate(columns, axis=0).astype(BF16)
    unit = (iota((LANES, LANES), 0) == iota((LANES, LANES), 1)).astype(F32).astype(BF16)
    chooser = lax.dot_general(
        unit, chosen, (((1,), (1,)), ((), ())), preferred_element_type=F32
    )[: 3 * tiles].astype(BF16)
    for copy in halo_copies[2:]:
        copy.wait()

    left, own, right_side = gather_back(0, chooser, (0, 1, 2))
    residual0 = residual0 + jnp.concatenate(own, axis=1)
    direction = residual0 * scale
    put(1, blocks_of(direction))
    scales = [unpack(halo_recv[side, 1]) for side in (0, 1)]
    directions = [
        [
            start + factor * back
            for start, factor, back in zip(unpack(halo_recv[side, 0]), scales[side], backs)
        ]
        for side, backs in ((0, left), (1, right_side))
    ]
    put(0, directions[0])
    put(2, directions[1])
    product1 = block_product(direction)
    image_send[...] = pack(product1 * scale)
    image_copies = []
    for side, delta in ((0, 1), (1, -1)):
        copy = pltpu.make_async_remote_copy(
            src_ref=image_send,
            dst_ref=image_recv.at[side],
            send_sem=image_send_sem.at[side],
            recv_sem=image_recv_sem.at[side],
            device_id=near(delta, 0),
            device_id_type=MESH,
        )
        copy.start()
        image_copies.append(copy)
    backward, _ = slot_rows()
    send_slots(1, backward)
    for copy in image_copies:
        copy.wait()
    left, own, right_side = gather_back(1, chooser, (0, 1, 2))
    image1 = product1 - jnp.concatenate(own, axis=1)
    trial = residual0 - image1
    shaped = trial * scale
    put(1, blocks_of(shaped))
    for side, backs in ((0, left), (1, right_side)):
        put(
            2 * side,
            [
                start - image + factor * back
                for start, image, factor, back in zip(
                    directions[side], unpack(image_recv[side]), scales[side], backs
                )
            ],
        )
    backward, energy = slot_rows()
    send_slots(2, backward)
    product2 = block_product(shaped)

    def lane_sum(field):
        total = field[:, :LANES]
        for i in range(1, pairs):
            total = total + field[:, i * LANES : (i + 1) * LANES]
        return jnp.sum(total, axis=0, keepdims=True) * (1.0 / grps)

    sums = jnp.zeros((ROWS, LANES), F32)
    for i, value in enumerate(
        (
            lane_sum(residual0 * direction),
            lane_sum(direction * image1),
            lane_sum(residual0 * shaped),
            lane_sum(trial * shaped),
            lane_sum(image1 * shaped),
            lane_sum(shaped * product2) - energy,
        )
    ):
        sums = jnp.where(row8 == i, value, sums)
    scalar_send[...] = sums

    def spread_scalars(i, carry):
        other = lax.rem(me + i, devices)
        pltpu.make_async_remote_copy(
            src_ref=scalar_send,
            dst_ref=scalar_recv.at[i - 1],
            send_sem=scalar_sem.at[0],
            recv_sem=scalar_sem.at[1],
            device_id=(other // grps, lax.rem(other, grps)),
            device_id_type=MESH,
        ).start()
        return carry

    lax.fori_loop(1, devices, spread_scalars, 0)
    (own,) = gather_back(2, chooser, (1,))
    image2 = product2 - jnp.concatenate(own, axis=1)
    wait_bytes(scalar_recv, scalar_sem.at[1])
    totals = jnp.sum(sums + jnp.sum(scalar_recv[...], axis=0), axis=1, keepdims=True)
    rz0, curve1, cross, trial_rz, mixed, curve_w = [totals[i : i + 1, :] for i in range(6)]
    step1 = rz0 / curve1
    short = 1.0 - step1
    rz1 = short * short * rz0 + 2.0 * short * step1 * cross + step1 * step1 * trial_rz
    keep = short + rz1 / rz0
    curve2 = keep * keep * curve1 + 2.0 * keep * step1 * mixed + step1 * step1 * curve_w
    step2 = rz1 / curve2
    near_part = step1 + step2 * keep
    far_part = step2 * step1
    solution_ref[...] = guess[...] + near_part * direction + far_part * shaped
    residual_ref[...] = residual0 - near_part * image1 - far_part * image2

    wait_bytes(scalar_recv, scalar_sem.at[0])
    wait_bytes(pattern_recv.at[others], pattern_sem.at[0])
    for turn_no in range(3):
        wait_bytes(slot_recv.at[turn_no, others], slot_send_sem.at[turn_no])


def per_device(
    cells, grps, initial_guess, right_side, camera_blocks, point_inverse, jacobian_tiles, tile_pattern, cell_load
):
    params, cameras = initial_guess.shape
    slots, rows_wide, points_wide = jacobian_tiles.shape
    chunks = (rows_wide + LANES - 1) // LANES
    near = SPAN * grps
    packed = cameras + LANES
    hbm = pl.BlockSpec(memory_space=pl.ANY)
    smem = pl.BlockSpec(memory_space=pltpu.SMEM)
    vmem = pl.BlockSpec(memory_space=pltpu.VMEM)
    dma = pltpu.SemaphoreType.DMA
    field = jax.ShapeDtypeStruct((params, cameras), F32)
    return pl.pallas_call(
        functools.partial(kernel, cells, grps),
        out_shape=(field, field),
        in_specs=[hbm] * 5 + [smem] * 2,
        out_specs=(vmem, vmem),
        scratch_shapes=[
            pltpu.VMEM((params, cameras), F32),
            pltpu.VMEM((params, cameras), F32),
            pltpu.VMEM(camera_blocks.shape, F32),
            pltpu.VMEM(point_inverse.shape, F32),
            pltpu.VMEM(jacobian_tiles.shape, BF16),
            pltpu.VMEM((3 * cameras // LANES, params, LANES), F32),
            pltpu.VMEM((ROWS, packed), BF16),
            pltpu.VMEM((2, ROWS, packed), BF16),
            pltpu.VMEM((2, ROWS, packed), F32),
            pltpu.VMEM((2, 2, ROWS, packed), F32),
            pltpu.VMEM((ROWS, packed), F32),
            pltpu.VMEM((2, ROWS, packed), F32),
            pltpu.VMEM((ROWS, LANES), jnp.int32),
            pltpu.VMEM((near, ROWS, LANES), jnp.int32),
            pltpu.VMEM((3, ROWS, chunks * LANES), BF16),
            pltpu.VMEM((3, near, ROWS, chunks * LANES), BF16),
            pltpu.VMEM((ROWS, LANES), F32),
            pltpu.VMEM((cells * grps - 1, ROWS, LANES), F32),
            dma((4,)),
            dma((slots,)),
            dma((2, 3)),
            dma((2, 3)),
            dma((2,)),
            dma((2,)),
            dma((2,)),
            dma((3,)),
            dma((3,)),
            dma((2,)),
        ],
        compiler_params=pltpu.CompilerParams(collective_id=0, has_side_effects=True),
    )(initial_guess, right_side, camera_blocks, point_inverse, jacobian_tiles, tile_pattern, cell_load)


def solution(mesh):
    placed = (
        P(None, "cell"),
        P(None, "cell"),
        P(None, None, "cell"),
        P(None, None, ("cell", "grp")),
        P(("cell", "grp"), None, None),
        P(("cell", "grp"), None),
        P("cell"),
    )
    return jax.shard_map(
        functools.partial(per_device, mesh.shape["cell"], mesh.shape["grp"]),
        mesh=mesh,
        in_specs=placed,
        out_specs=(P(None, "cell"), P(None, "cell")),
        check_vma=False,
    )
```

```python
import functools

import jax
import jax.numpy as jnp
from jax import lax
from jax.experimental import pallas as pl
from jax.experimental.pallas import tpu as pltpu
from jax.sharding import PartitionSpec as P

CAM_TILE = 64
ITERS = 2
REACH = 2
SPAN = 2 * REACH + 1
ORDER = sorted(range(-REACH, REACH + 1), key=abs)
LANES = 128
ROWS = 8
MESH = pl.DeviceIdType.MESH
F32 = jnp.float32
BF16 = jnp.bfloat16


def kernel(
    cells,
    grps,
    guess_hbm,
    right_hbm,
    blocks_hbm,
    inverse_hbm,
    jac_hbm,
    pattern,
    load,
    solution_ref,
    residual_ref,
    guess,
    right,
    blocks,
    inverse,
    jac,
    window,
    guess_send,
    guess_recv,
    halo_send,
    halo_recv,
    image_send,
    image_recv,
    pattern_send,
    pattern_recv,
    slot_send,
    slot_recv,
    scalar_send,
    scalar_recv,
    local_sem,
    jac_sem,
    halo_send_sem,
    halo_recv_sem,
    image_send_sem,
    image_recv_sem,
    pattern_sem,
    slot_send_sem,
    slot_recv_sem,
    scalar_sem,
):
    params, cameras = guess.shape
    slots, rows_wide, points_wide = jac.shape
    tiles = cameras // CAM_TILE
    pairs = cameras // LANES
    coords = inverse.shape[0]
    point_tiles = inverse.shape[2] // LANES
    devices = cells * grps
    cell = lax.axis_index("cell")
    grp = lax.axis_index("grp")
    me = cell * grps + grp

    local = [
        pltpu.make_async_copy(src, dst, local_sem.at[i])
        for i, (src, dst) in enumerate(
            ((guess_hbm, guess), (blocks_hbm, blocks), (right_hbm, right), (inverse_hbm, inverse))
        )
    ]
    jac_copies = [
        pltpu.make_async_copy(jac_hbm.at[s], jac.at[s], jac_sem.at[s]) for s in range(slots)
    ]
    for copy in local:
        copy.start()
    for copy in jac_copies:
        copy.start()

    barrier = pltpu.get_barrier_semaphore()

    def greet(i, carry):
        other = lax.rem(me + i, devices)
        pl.semaphore_signal(
            barrier, inc=1, device_id=(other // grps, lax.rem(other, grps)), device_id_type=MESH
        )
        return carry

    lax.fori_loop(1, devices, greet, 0)

    def near(delta, turn):
        return (lax.rem(cell + delta + cells, cells), lax.rem(grp + turn, grps))

    def slot_index(delta, turn):
        return ORDER.index(delta) * grps + turn % grps

    def peers(reach):
        found = []
        for delta in sorted(range(-reach, reach + 1), key=abs):
            for turn in range(grps):
                if delta != 0 or turn != 0:
                    found.append((delta, turn))
        return found

    def iota(shape, axis):
        return lax.broadcasted_iota(jnp.int32, shape, axis)

    lane8 = iota((ROWS, LANES), 1)
    row8 = iota((ROWS, LANES), 0)
    lane9 = iota((params, LANES), 1)
    row9 = iota((params, LANES), 0)
    low9 = lane9 < CAM_TILE
    chunks = (rows_wide + LANES - 1) // LANES
    own_rows = [row9 == 2 * b + (lane9 >= CAM_TILE).astype(jnp.int32) for b in range(chunks)]

    live = [s < load[0] for s in range(slots)]
    ids = [pattern[0, s] for s in range(slots)]
    point_ids = [pattern[1, s] for s in range(slots)]
    id_rows = jnp.full((ROWS, LANES), -4096, jnp.int32)
    point_rows = jnp.full((ROWS, LANES), -1, jnp.int32)
    for s in range(slots):
        id_rows = jnp.where(row8 == s, jnp.where(live[s], ids[s], -4096), id_rows)
        point_rows = jnp.where(row8 == s, point_ids[s], point_rows)
    pattern_send[...] = id_rows
    pattern_recv[0] = id_rows

    def pack(field):
        tail = jnp.zeros((ROWS, LANES), F32)
        for i in range(pairs):
            tail = jnp.where(row8 == i, field[ROWS:, i * LANES : (i + 1) * LANES], tail)
        return jnp.concatenate([field[:ROWS], tail], axis=1)

    def unpack(packed):
        return [
            jnp.concatenate(
                [packed[:, i * LANES : (i + 1) * LANES], packed[i : i + 1, cameras:]], axis=0
            )
            for i in range(pairs)
        ]

    def blocks_of(field):
        return [field[:, i * LANES : (i + 1) * LANES] for i in range(pairs)]

    local[0].wait()
    guess_send[...] = pack(guess[...]).astype(BF16)
    local[1].wait()

    def block_product(field):
        total = blocks[0] * field[0:1, :]
        for k in range(1, params):
            total = total + blocks[k] * field[k : k + 1, :]
        return total

    row_wide = iota((params, cameras), 0)
    diagonal = blocks[0]
    for k in range(1, params):
        diagonal = jnp.where(row_wide == k, blocks[k], diagonal)
    scale = 1.0 / diagonal
    local[2].wait()
    residual0 = right[...] - block_product(guess[...])
    halo_send[0] = pack(residual0 * scale)
    halo_send[1] = pack(scale)
    local[3].wait()
    inverse_rows = []
    for j in range(coords):
        for i in range(coords):
            picked = jnp.zeros((ROWS, LANES), F32)
            for q in range(point_tiles):
                picked = jnp.where(
                    point_rows == q, inverse[j, i : i + 1, q * LANES : (q + 1) * LANES], picked
                )
            inverse_rows.append(picked)
    pad = jnp.zeros((ROWS, chunks * LANES - rows_wide), F32)

    pl.semaphore_wait(barrier, devices - 1)

    halo_copies = []
    for part in range(3):
        for side, delta in ((0, 1), (1, -1)):
            copy = pltpu.make_async_remote_copy(
                src_ref=guess_send if part == 0 else halo_send.at[part - 1],
                dst_ref=guess_recv.at[side] if part == 0 else halo_recv.at[side, part - 1],
                send_sem=halo_send_sem.at[side, part],
                recv_sem=halo_recv_sem.at[side, part],
                device_id=near(delta, 0),
                device_id_type=MESH,
            )
            halo_copies.append(copy)
    halo_copies[0].start()
    halo_copies[1].start()
    for delta, turn in peers(REACH):
        pltpu.make_async_remote_copy(
            src_ref=pattern_send,
            dst_ref=pattern_recv.at[slot_index(-delta, -turn)],
            send_sem=pattern_sem.at[0],
            recv_sem=pattern_sem.at[1],
            device_id=near(delta, turn),
            device_id_type=MESH,
        ).start()
    for copy in halo_copies[2:]:
        copy.start()

    def put(side, parts):
        for i in range(pairs):
            window[side * pairs + i] = parts[i]

    def slot_rows():
        forward = jnp.zeros((ROWS, points_wide), F32)
        row_points = iota((ROWS, points_wide), 0)
        for s in range(slots):
            block = window[lax.shift_right_logical(ids[s], 1)]
            turned = pltpu.roll(block, CAM_TILE, 1)
            odd = lax.bitwise_and(ids[s], 1)
            keep = jnp.where(low9, 0, 1) == odd
            tile = jnp.where(keep, block, turned)
            tile = jnp.where(live[s], tile, 0.0)
            spread = jnp.concatenate([jnp.where(own, tile, 0.0) for own in own_rows], axis=1)
            left = spread[:, :rows_wide].astype(BF16)
            product = jnp.dot(left, jac[s], preferred_element_type=F32)
            total = jnp.sum(product, axis=0, keepdims=True)
            forward = jnp.where(row_points == s, total, forward)
        wide_points = jnp.concatenate([point_rows] * coords, axis=1)
        sums = jnp.zeros((ROWS, points_wide), F32)
        for s in range(slots):
            sums = sums + jnp.where(wide_points == point_ids[s], forward[s : s + 1, :], 0.0)
        solved = []
        for j in range(coords):
            total = inverse_rows[j * coords] * sums[:, :LANES]
            for i in range(1, coords):
                total = total + inverse_rows[j * coords + i] * sums[:, i * LANES : (i + 1) * LANES]
            solved.append(total)
        solved = jnp.concatenate(solved, axis=1).astype(BF16)
        energy = forward * solved.astype(F32)
        backward = jnp.zeros((ROWS, rows_wide), F32)
        row_cams = iota((ROWS, rows_wide), 0)
        for s in range(slots):
            product = lax.dot_general(
                solved, jac[s], (((1,), (1,)), ((), ())), preferred_element_type=F32
            )
            backward = jnp.where(row_cams == s, jnp.where(live[s], product, 0.0), backward)
        backward = jnp.concatenate([backward, pad], axis=1).astype(BF16)
        energy_lanes = energy[:, :LANES]
        for i in range(1, coords):
            energy_lanes = energy_lanes + energy[:, i * LANES : (i + 1) * LANES]
        return backward, jnp.sum(energy_lanes, axis=0, keepdims=True)

    def send_slots(turn_no, backward, reach):
        slot_send[turn_no] = backward
        slot_recv[turn_no, 0] = backward
        for delta, turn in peers(reach):
            pltpu.make_async_remote_copy(
                src_ref=slot_send.at[turn_no],
                dst_ref=slot_recv.at[turn_no, slot_index(-delta, -turn)],
                send_sem=slot_send_sem.at[turn_no],
                recv_sem=slot_recv_sem.at[turn_no],
                device_id=near(delta, turn),
                device_id_type=MESH,
            ).start()

    others = pl.ds(1, SPAN * grps - 1)
    closer = pl.ds(1, 3 * grps - 1)

    def wait_bytes(ref, sem):
        pltpu.make_async_copy(ref, ref, sem).wait()

    def gather_back(turn_no, chooser, sides, count):
        wait_bytes(slot_recv.at[turn_no, pl.ds(1, count - 1)], slot_recv_sem.at[turn_no])
        height = count * ROWS
        stacked = slot_recv[turn_no, :count].astype(F32).reshape(height, chunks * LANES)
        summed = jnp.dot(
            chooser[:, :height], stacked.astype(BF16), preferred_element_type=F32
        )
        fields = []
        for side in sides:
            parts = []
            for i in range(pairs):
                first = side * tiles + 2 * i
                both = []
                for t in (first, first + 1):
                    total = jnp.zeros((params, LANES), F32)
                    for b in range(chunks):
                        piece = summed[t : t + 1, b * LANES : (b + 1) * LANES]
                        total = jnp.where(own_rows[b], piece, total)
                    both.append(total)
                parts.append(
                    jnp.where(low9, both[0], both[1])
                    + pltpu.roll(jnp.where(low9, both[1], both[0]), CAM_TILE, 1)
                )
            fields.append(parts)
        return fields

    put(1, blocks_of(guess[...]))
    halo_copies[0].wait()
    halo_copies[1].wait()
    put(0, unpack(guess_recv[0].astype(F32)))
    put(2, unpack(guess_recv[1].astype(F32)))
    for copy in jac_copies:
        copy.wait()
    backward, _ = slot_rows()
    send_slots(0, backward, REACH)

    wait_bytes(pattern_recv.at[others], pattern_sem.at[1])
    columns = []
    for shift, delta in enumerate(ORDER):
        for turn in range(grps):
            at = pattern_recv[shift * grps + turn] + delta * tiles
            columns.append((at == lane8).astype(F32))
    chosen = jnp.concatenate(columns, axis=0).astype(BF16)
    unit = (iota((LANES, LANES), 0) == iota((LANES, LANES), 1)).astype(F32).astype(BF16)
    chooser = lax.dot_general(
        unit, chosen, (((1,), (1,)), ((), ())), preferred_element_type=F32
    )[: 3 * tiles].astype(BF16)
    for copy in halo_copies[2:]:
        copy.wait()

    left, own, right_side = gather_back(0, chooser, (0, 1, 2), SPAN * grps)
    residual0 = residual0 + jnp.concatenate(own, axis=1)
    direction = residual0 * scale
    put(1, blocks_of(direction))
    scales = [unpack(halo_recv[side, 1]) for side in (0, 1)]
    directions = [
        [
            start + factor * back
            for start, factor, back in zip(unpack(halo_recv[side, 0]), scales[side], backs)
        ]
        for side, backs in ((0, left), (1, right_side))
    ]
    put(0, directions[0])
    put(2, directions[1])
    product1 = block_product(direction)
    image_send[...] = pack(product1 * scale)
    image_copies = []
    for side, delta in ((0, 1), (1, -1)):
        copy = pltpu.make_async_remote_copy(
            src_ref=image_send,
            dst_ref=image_recv.at[side],
            send_sem=image_send_sem.at[side],
            recv_sem=image_recv_sem.at[side],
            device_id=near(delta, 0),
            device_id_type=MESH,
        )
        copy.start()
        image_copies.append(copy)
    backward, _ = slot_rows()
    send_slots(1, backward, REACH)
    for copy in image_copies:
        copy.wait()
    left, own, right_side = gather_back(1, chooser, (0, 1, 2), SPAN * grps)
    image1 = product1 - jnp.concatenate(own, axis=1)
    trial = residual0 - image1
    shaped = trial * scale
    put(1, blocks_of(shaped))
    for side, backs in ((0, left), (1, right_side)):
        put(
            2 * side,
            [
                start - image + factor * back
                for start, image, factor, back in zip(
                    directions[side], unpack(image_recv[side]), scales[side], backs
                )
            ],
        )
    backward, energy = slot_rows()
    send_slots(2, backward, 1)
    product2 = block_product(shaped)

    def lane_sum(field):
        total = field[:, :LANES]
        for i in range(1, pairs):
            total = total + field[:, i * LANES : (i + 1) * LANES]
        return jnp.sum(total, axis=0, keepdims=True) * (1.0 / grps)

    sums = jnp.zeros((ROWS, LANES), F32)
    for i, value in enumerate(
        (
            lane_sum(residual0 * direction),
            lane_sum(direction * image1),
            lane_sum(residual0 * shaped),
            lane_sum(trial * shaped),
            lane_sum(image1 * shaped),
            lane_sum(shaped * product2) - energy,
        )
    ):
        sums = jnp.where(row8 == i, value, sums)
    scalar_send[...] = sums

    def spread_scalars(i, carry):
        other = lax.rem(me + i, devices)
        pltpu.make_async_remote_copy(
            src_ref=scalar_send,
            dst_ref=scalar_recv.at[i - 1],
            send_sem=scalar_sem.at[0],
            recv_sem=scalar_sem.at[1],
            device_id=(other // grps, lax.rem(other, grps)),
            device_id_type=MESH,
        ).start()
        return carry

    lax.fori_loop(1, devices, spread_scalars, 0)
    (own,) = gather_back(2, chooser, (1,), 3 * grps)
    image2 = product2 - jnp.concatenate(own, axis=1)
    wait_bytes(scalar_recv, scalar_sem.at[1])
    totals = jnp.sum(sums + jnp.sum(scalar_recv[...], axis=0), axis=1, keepdims=True)
    rz0, curve1, cross, trial_rz, mixed, curve_w = [totals[i : i + 1, :] for i in range(6)]
    step1 = rz0 / curve1
    short = 1.0 - step1
    rz1 = short * short * rz0 + 2.0 * short * step1 * cross + step1 * step1 * trial_rz
    keep = short + rz1 / rz0
    curve2 = keep * keep * curve1 + 2.0 * keep * step1 * mixed + step1 * step1 * curve_w
    step2 = rz1 / curve2
    near_part = step1 + step2 * keep
    far_part = step2 * step1
    solution_ref[...] = guess[...] + near_part * direction + far_part * shaped
    residual_ref[...] = residual0 - near_part * image1 - far_part * image2

    wait_bytes(scalar_recv, scalar_sem.at[0])
    wait_bytes(pattern_recv.at[others], pattern_sem.at[0])
    for turn_no, sent in enumerate((others, others, closer)):
        wait_bytes(slot_recv.at[turn_no, sent], slot_send_sem.at[turn_no])


def finish_kernel(first, second, solution_ref, residual_ref):
    solution_ref[...] = first[...]
    residual_ref[...] = second[...]


def finish(first, second):
    vmem = pl.BlockSpec(memory_space=pltpu.VMEM)
    shape = jax.ShapeDtypeStruct(first.shape, first.dtype)
    return pl.pallas_call(
        finish_kernel, out_shape=(shape, shape), in_specs=[vmem] * 2, out_specs=(vmem, vmem)
    )(first, second)


def per_device(
    cells, grps, initial_guess, right_side, camera_blocks, point_inverse, jacobian_tiles, tile_pattern, cell_load
):
    params, cameras = initial_guess.shape
    slots, rows_wide, points_wide = jacobian_tiles.shape
    chunks = (rows_wide + LANES - 1) // LANES
    near = SPAN * grps
    packed = cameras + LANES
    hbm = pl.BlockSpec(memory_space=pl.ANY)
    smem = pl.BlockSpec(memory_space=pltpu.SMEM)
    vmem = pl.BlockSpec(memory_space=pltpu.VMEM)
    dma = pltpu.SemaphoreType.DMA
    field = jax.ShapeDtypeStruct((params, cameras), F32)
    first, second = pl.pallas_call(
        functools.partial(kernel, cells, grps),
        out_shape=(field, field),
        in_specs=[hbm] * 5 + [smem] * 2,
        out_specs=(vmem, vmem),
        scratch_shapes=[
            pltpu.VMEM((params, cameras), F32),
            pltpu.VMEM((params, cameras), F32),
            pltpu.VMEM(camera_blocks.shape, F32),
            pltpu.VMEM(point_inverse.shape, F32),
            pltpu.VMEM(jacobian_tiles.shape, BF16),
            pltpu.VMEM((3 * cameras // LANES, params, LANES), F32),
            pltpu.VMEM((ROWS, packed), BF16),
            pltpu.VMEM((2, ROWS, packed), BF16),
            pltpu.VMEM((2, ROWS, packed), F32),
            pltpu.VMEM((2, 2, ROWS, packed), F32),
            pltpu.VMEM((ROWS, packed), F32),
            pltpu.VMEM((2, ROWS, packed), F32),
            pltpu.VMEM((ROWS, LANES), jnp.int32),
            pltpu.VMEM((near, ROWS, LANES), jnp.int32),
            pltpu.VMEM((3, ROWS, chunks * LANES), BF16),
            pltpu.VMEM((3, near, ROWS, chunks * LANES), BF16),
            pltpu.VMEM((ROWS, LANES), F32),
            pltpu.VMEM((cells * grps - 1, ROWS, LANES), F32),
            dma((4,)),
            dma((slots,)),
            dma((2, 3)),
            dma((2, 3)),
            dma((2,)),
            dma((2,)),
            dma((2,)),
            dma((3,)),
            dma((3,)),
            dma((2,)),
        ],
        compiler_params=pltpu.CompilerParams(collective_id=0, has_side_effects=True),
    )(initial_guess, right_side, camera_blocks, point_inverse, jacobian_tiles, tile_pattern.T, cell_load)
    return finish(first, second)


def solution(mesh):
    placed = (
        P(None, "cell"),
        P(None, "cell"),
        P(None, None, "cell"),
        P(None, None, ("cell", "grp")),
        P(("cell", "grp"), None, None),
        P(("cell", "grp"), None),
        P("cell"),
    )
    return jax.shard_map(
        functools.partial(per_device, mesh.shape["cell"], mesh.shape["grp"]),
        mesh=mesh,
        in_specs=placed,
        out_specs=(P(None, "cell"), P(None, "cell")),
        check_vma=False,
    )
```

```python
import functools

import jax
import jax.numpy as jnp
from jax import lax
from jax.experimental import pallas as pl
from jax.experimental.pallas import tpu as pltpu
from jax.sharding import PartitionSpec as P

CAM_TILE = 64
ITERS = 2
REACH = 2
SPAN = 2 * REACH + 1
ORDER = sorted(range(-REACH, REACH + 1), key=abs)
LANES = 128
ROWS = 8
MESH = pl.DeviceIdType.MESH
F32 = jnp.float32
BF16 = jnp.bfloat16


def kernel(
    cells,
    grps,
    guess_hbm,
    right_hbm,
    blocks_hbm,
    inverse_hbm,
    jac_hbm,
    pattern,
    load,
    solution_ref,
    residual_ref,
    guess,
    right,
    blocks,
    inverse,
    jac,
    window,
    guess_send,
    guess_recv,
    halo_send,
    halo_recv,
    image_send,
    image_recv,
    pattern_send,
    pattern_recv,
    slot_send,
    slot_recv,
    scalar_send,
    scalar_recv,
    local_sem,
    jac_sem,
    halo_send_sem,
    halo_recv_sem,
    image_send_sem,
    image_recv_sem,
    pattern_sem,
    slot_send_sem,
    slot_recv_sem,
    scalar_sem,
):
    params, cameras = guess.shape
    slots, rows_wide, points_wide = jac.shape
    tiles = cameras // CAM_TILE
    pairs = cameras // LANES
    coords = inverse.shape[0]
    point_tiles = inverse.shape[2] // LANES
    devices = cells * grps
    cell = lax.axis_index("cell")
    grp = lax.axis_index("grp")

    local = [
        pltpu.make_async_copy(src, dst, local_sem.at[i])
        for i, (src, dst) in enumerate(
            ((guess_hbm, guess), (blocks_hbm, blocks), (right_hbm, right), (inverse_hbm, inverse))
        )
    ]
    jac_copies = [
        pltpu.make_async_copy(jac_hbm.at[s], jac.at[s], jac_sem.at[s]) for s in range(slots)
    ]
    for copy in local:
        copy.start()
    for copy in jac_copies:
        copy.start()

    barrier = pltpu.get_barrier_semaphore()

    turned = [lax.rem(grp + turn, grps) for turn in range(grps)]

    def everyone(act):
        for turn in range(1, grps):
            act(turn - 1, (cell, turned[turn]))

        def one_cell(delta, carry):
            other = lax.rem(cell + delta, cells)
            for turn in range(grps):
                act(delta * grps + (turn - 1), (other, turned[turn]))
            return carry

        lax.fori_loop(1, cells, one_cell, 0)

    def greet(index, device):
        pl.semaphore_signal(barrier, inc=1, device_id=device, device_id_type=MESH)

    everyone(greet)

    def near(delta, turn):
        return (lax.rem(cell + delta + cells, cells), lax.rem(grp + turn, grps))

    def slot_index(delta, turn):
        return ORDER.index(delta) * grps + turn % grps

    def peers(reach):
        found = []
        for delta in sorted(range(-reach, reach + 1), key=abs):
            for turn in range(grps):
                if delta != 0 or turn != 0:
                    found.append((delta, turn))
        return sorted(found, key=lambda peer: (abs(peer[0]), -peer[1]))

    def iota(shape, axis):
        return lax.broadcasted_iota(jnp.int32, shape, axis)

    lane8 = iota((ROWS, LANES), 1)
    row8 = iota((ROWS, LANES), 0)
    lane9 = iota((params, LANES), 1)
    row9 = iota((params, LANES), 0)
    low9 = lane9 < CAM_TILE
    chunks = (rows_wide + LANES - 1) // LANES
    own_rows = [row9 == 2 * b + (lane9 >= CAM_TILE).astype(jnp.int32) for b in range(chunks)]

    live = [s < load[0] for s in range(slots)]
    ids = [pattern[0, s] for s in range(slots)]
    point_ids = [pattern[1, s] for s in range(slots)]
    id_rows = jnp.full((ROWS, LANES), -4096, jnp.int32)
    point_rows = jnp.full((ROWS, LANES), -1, jnp.int32)
    for s in range(slots):
        id_rows = jnp.where(row8 == s, jnp.where(live[s], ids[s], -4096), id_rows)
        point_rows = jnp.where(row8 == s, point_ids[s], point_rows)
    pattern_send[...] = id_rows
    pattern_recv[0] = id_rows

    def pack(field):
        tail = jnp.zeros((ROWS, LANES), F32)
        for i in range(pairs):
            tail = jnp.where(row8 == i, field[ROWS:, i * LANES : (i + 1) * LANES], tail)
        return jnp.concatenate([field[:ROWS], tail], axis=1)

    def unpack(packed):
        return [
            jnp.concatenate(
                [packed[:, i * LANES : (i + 1) * LANES], packed[i : i + 1, cameras:]], axis=0
            )
            for i in range(pairs)
        ]

    def blocks_of(field):
        return [field[:, i * LANES : (i + 1) * LANES] for i in range(pairs)]

    local[0].wait()
    guess_send[...] = pack(guess[...]).astype(BF16)
    local[1].wait()

    def block_product(field):
        total = blocks[0] * field[0:1, :]
        for k in range(1, params):
            total = total + blocks[k] * field[k : k + 1, :]
        return total

    row_wide = iota((params, cameras), 0)
    diagonal = blocks[0]
    for k in range(1, params):
        diagonal = jnp.where(row_wide == k, blocks[k], diagonal)
    scale = 1.0 / diagonal
    local[2].wait()
    residual0 = right[...] - block_product(guess[...])
    halo_send[0] = pack(residual0 * scale)
    halo_send[1] = pack(scale)
    local[3].wait()
    inverse_rows = []
    for j in range(coords):
        for i in range(coords):
            picked = jnp.zeros((ROWS, LANES), F32)
            for q in range(point_tiles):
                picked = jnp.where(
                    point_rows == q, inverse[j, i : i + 1, q * LANES : (q + 1) * LANES], picked
                )
            inverse_rows.append(picked)
    pad = jnp.zeros((ROWS, chunks * LANES - rows_wide), F32)

    pl.semaphore_wait(barrier, devices - 1)

    halo_copies = []
    for part in range(3):
        for side, delta in ((0, 1), (1, -1)):
            copy = pltpu.make_async_remote_copy(
                src_ref=guess_send if part == 0 else halo_send.at[part - 1],
                dst_ref=guess_recv.at[side] if part == 0 else halo_recv.at[side, part - 1],
                send_sem=halo_send_sem.at[side, part],
                recv_sem=halo_recv_sem.at[side, part],
                device_id=near(delta, 0),
                device_id_type=MESH,
            )
            halo_copies.append(copy)
    halo_copies[0].start()
    halo_copies[1].start()
    for delta, turn in peers(REACH):
        pltpu.make_async_remote_copy(
            src_ref=pattern_send,
            dst_ref=pattern_recv.at[slot_index(-delta, -turn)],
            send_sem=pattern_sem.at[0],
            recv_sem=pattern_sem.at[1],
            device_id=near(delta, turn),
            device_id_type=MESH,
        ).start()
    for copy in halo_copies[2:]:
        copy.start()

    def put(side, parts):
        for i in range(pairs):
            window[side * pairs + i] = parts[i]

    def slot_rows():
        forward = jnp.zeros((ROWS, points_wide), F32)
        row_points = iota((ROWS, points_wide), 0)
        for s in range(slots):
            block = window[lax.shift_right_logical(ids[s], 1)]
            turned = pltpu.roll(block, CAM_TILE, 1)
            odd = lax.bitwise_and(ids[s], 1)
            keep = jnp.where(low9, 0, 1) == odd
            tile = jnp.where(keep, block, turned)
            tile = jnp.where(live[s], tile, 0.0)
            spread = jnp.concatenate([jnp.where(own, tile, 0.0) for own in own_rows], axis=1)
            left = spread[:, :rows_wide].astype(BF16)
            product = jnp.dot(left, jac[s], preferred_element_type=F32)
            total = jnp.sum(product, axis=0, keepdims=True)
            forward = jnp.where(row_points == s, total, forward)
        wide_points = jnp.concatenate([point_rows] * coords, axis=1)
        sums = jnp.zeros((ROWS, points_wide), F32)
        for s in range(slots):
            sums = sums + jnp.where(wide_points == point_ids[s], forward[s : s + 1, :], 0.0)
        solved = []
        for j in range(coords):
            total = inverse_rows[j * coords] * sums[:, :LANES]
            for i in range(1, coords):
                total = total + inverse_rows[j * coords + i] * sums[:, i * LANES : (i + 1) * LANES]
            solved.append(total)
        solved = jnp.concatenate(solved, axis=1).astype(BF16)
        energy = forward * solved.astype(F32)
        backward = jnp.zeros((ROWS, rows_wide), F32)
        row_cams = iota((ROWS, rows_wide), 0)
        for s in range(slots):
            product = lax.dot_general(
                solved, jac[s], (((1,), (1,)), ((), ())), preferred_element_type=F32
            )
            backward = jnp.where(row_cams == s, jnp.where(live[s], product, 0.0), backward)
        backward = jnp.concatenate([backward, pad], axis=1).astype(BF16)
        energy_lanes = energy[:, :LANES]
        for i in range(1, coords):
            energy_lanes = energy_lanes + energy[:, i * LANES : (i + 1) * LANES]
        return backward, jnp.sum(energy_lanes, axis=0, keepdims=True)

    def send_slots(turn_no, backward, reach):
        slot_send[turn_no] = backward
        slot_recv[turn_no, 0] = backward
        for delta, turn in peers(reach):
            pltpu.make_async_remote_copy(
                src_ref=slot_send.at[turn_no],
                dst_ref=slot_recv.at[turn_no, slot_index(-delta, -turn)],
                send_sem=slot_send_sem.at[turn_no],
                recv_sem=slot_recv_sem.at[turn_no],
                device_id=near(delta, turn),
                device_id_type=MESH,
            ).start()

    others = pl.ds(1, SPAN * grps - 1)
    closer = pl.ds(1, 3 * grps - 1)

    def wait_bytes(ref, sem):
        pltpu.make_async_copy(ref, ref, sem).wait()

    def gather_back(turn_no, chooser, sides, count):
        wait_bytes(slot_recv.at[turn_no, pl.ds(1, count - 1)], slot_recv_sem.at[turn_no])
        height = count * ROWS
        stacked = slot_recv[turn_no, :count].astype(F32).reshape(height, chunks * LANES)
        summed = jnp.dot(
            chooser[:, :height], stacked.astype(BF16), preferred_element_type=F32
        )
        fields = []
        for side in sides:
            parts = []
            for i in range(pairs):
                first = side * tiles + 2 * i
                both = []
                for t in (first, first + 1):
                    total = jnp.zeros((params, LANES), F32)
                    for b in range(chunks):
                        piece = summed[t : t + 1, b * LANES : (b + 1) * LANES]
                        total = jnp.where(own_rows[b], piece, total)
                    both.append(total)
                parts.append(
                    jnp.where(low9, both[0], both[1])
                    + pltpu.roll(jnp.where(low9, both[1], both[0]), CAM_TILE, 1)
                )
            fields.append(parts)
        return fields

    put(1, blocks_of(guess[...]))
    halo_copies[0].wait()
    halo_copies[1].wait()
    put(0, unpack(guess_recv[0].astype(F32)))
    put(2, unpack(guess_recv[1].astype(F32)))
    for copy in jac_copies:
        copy.wait()
    backward, _ = slot_rows()
    send_slots(0, backward, REACH)

    wait_bytes(pattern_recv.at[others], pattern_sem.at[1])
    columns = []
    for shift, delta in enumerate(ORDER):
        for turn in range(grps):
            at = pattern_recv[shift * grps + turn] + delta * tiles
            columns.append((at == lane8).astype(F32))
    chosen = jnp.concatenate(columns, axis=0).astype(BF16)
    unit = (iota((LANES, LANES), 0) == iota((LANES, LANES), 1)).astype(F32).astype(BF16)
    chooser = lax.dot_general(
        unit, chosen, (((1,), (1,)), ((), ())), preferred_element_type=F32
    )[: 3 * tiles].astype(BF16)
    for copy in halo_copies[2:]:
        copy.wait()

    left, own, right_side = gather_back(0, chooser, (0, 1, 2), SPAN * grps)
    residual0 = residual0 + jnp.concatenate(own, axis=1)
    direction = residual0 * scale
    put(1, blocks_of(direction))
    scales = [unpack(halo_recv[side, 1]) for side in (0, 1)]
    directions = [
        [
            start + factor * back
            for start, factor, back in zip(unpack(halo_recv[side, 0]), scales[side], backs)
        ]
        for side, backs in ((0, left), (1, right_side))
    ]
    put(0, directions[0])
    put(2, directions[1])
    product1 = block_product(direction)
    image_send[...] = pack(product1 * scale)
    image_copies = []
    for side, delta in ((0, 1), (1, -1)):
        copy = pltpu.make_async_remote_copy(
            src_ref=image_send,
            dst_ref=image_recv.at[side],
            send_sem=image_send_sem.at[side],
            recv_sem=image_recv_sem.at[side],
            device_id=near(delta, 0),
            device_id_type=MESH,
        )
        copy.start()
        image_copies.append(copy)
    backward, _ = slot_rows()
    send_slots(1, backward, REACH)
    for copy in image_copies:
        copy.wait()
    left, own, right_side = gather_back(1, chooser, (0, 1, 2), SPAN * grps)
    image1 = product1 - jnp.concatenate(own, axis=1)
    trial = residual0 - image1
    shaped = trial * scale
    put(1, blocks_of(shaped))
    for side, backs in ((0, left), (1, right_side)):
        put(
            2 * side,
            [
                start - image + factor * back
                for start, image, factor, back in zip(
                    directions[side], unpack(image_recv[side]), scales[side], backs
                )
            ],
        )
    backward, energy = slot_rows()
    send_slots(2, backward, 1)
    product2 = block_product(shaped)

    def lane_sum(field):
        total = field[:, :LANES]
        for i in range(1, pairs):
            total = total + field[:, i * LANES : (i + 1) * LANES]
        return jnp.sum(total, axis=0, keepdims=True) * (1.0 / grps)

    sums = jnp.zeros((ROWS, LANES), F32)
    for i, value in enumerate(
        (
            lane_sum(residual0 * direction),
            lane_sum(direction * image1),
            lane_sum(residual0 * shaped),
            lane_sum(trial * shaped),
            lane_sum(image1 * shaped),
            lane_sum(shaped * product2) - energy,
        )
    ):
        sums = jnp.where(row8 == i, value, sums)
    scalar_send[...] = sums

    def send_scalars(index, device):
        pltpu.make_async_remote_copy(
            src_ref=scalar_send,
            dst_ref=scalar_recv.at[index],
            send_sem=scalar_sem.at[0],
            recv_sem=scalar_sem.at[1],
            device_id=device,
            device_id_type=MESH,
        ).start()

    everyone(send_scalars)
    (own,) = gather_back(2, chooser, (1,), 3 * grps)
    image2 = product2 - jnp.concatenate(own, axis=1)
    wait_bytes(scalar_recv, scalar_sem.at[1])
    totals = jnp.sum(sums + jnp.sum(scalar_recv[...], axis=0), axis=1, keepdims=True)
    rz0, curve1, cross, trial_rz, mixed, curve_w = [totals[i : i + 1, :] for i in range(6)]
    step1 = rz0 / curve1
    short = 1.0 - step1
    rz1 = short * short * rz0 + 2.0 * short * step1 * cross + step1 * step1 * trial_rz
    keep = short + rz1 / rz0
    curve2 = keep * keep * curve1 + 2.0 * keep * step1 * mixed + step1 * step1 * curve_w
    step2 = rz1 / curve2
    near_part = step1 + step2 * keep
    far_part = step2 * step1
    solution_ref[...] = guess[...] + near_part * direction + far_part * shaped
    residual_ref[...] = residual0 - near_part * image1 - far_part * image2

    wait_bytes(scalar_recv, scalar_sem.at[0])
    wait_bytes(pattern_recv.at[others], pattern_sem.at[0])
    for turn_no, sent in enumerate((others, others, closer)):
        wait_bytes(slot_recv.at[turn_no, sent], slot_send_sem.at[turn_no])


def finish_kernel(first, second, solution_ref, residual_ref):
    solution_ref[...] = first[...]
    residual_ref[...] = second[...]


def finish(first, second):
    vmem = pl.BlockSpec(memory_space=pltpu.VMEM)
    shape = jax.ShapeDtypeStruct(first.shape, first.dtype)
    return pl.pallas_call(
        finish_kernel, out_shape=(shape, shape), in_specs=[vmem] * 2, out_specs=(vmem, vmem)
    )(first, second)


def per_device(
    cells, grps, initial_guess, right_side, camera_blocks, point_inverse, jacobian_tiles, tile_pattern, cell_load
):
    params, cameras = initial_guess.shape
    slots, rows_wide, points_wide = jacobian_tiles.shape
    chunks = (rows_wide + LANES - 1) // LANES
    near = SPAN * grps
    packed = cameras + LANES
    hbm = pl.BlockSpec(memory_space=pl.ANY)
    smem = pl.BlockSpec(memory_space=pltpu.SMEM)
    vmem = pl.BlockSpec(memory_space=pltpu.VMEM)
    dma = pltpu.SemaphoreType.DMA
    field = jax.ShapeDtypeStruct((params, cameras), F32)
    first, second = pl.pallas_call(
        functools.partial(kernel, cells, grps),
        out_shape=(field, field),
        in_specs=[hbm] * 5 + [smem] * 2,
        out_specs=(vmem, vmem),
        scratch_shapes=[
            pltpu.VMEM((params, cameras), F32),
            pltpu.VMEM((params, cameras), F32),
            pltpu.VMEM(camera_blocks.shape, F32),
            pltpu.VMEM(point_inverse.shape, F32),
            pltpu.VMEM(jacobian_tiles.shape, BF16),
            pltpu.VMEM((3 * cameras // LANES, params, LANES), F32),
            pltpu.VMEM((ROWS, packed), BF16),
            pltpu.VMEM((2, ROWS, packed), BF16),
            pltpu.VMEM((2, ROWS, packed), F32),
            pltpu.VMEM((2, 2, ROWS, packed), F32),
            pltpu.VMEM((ROWS, packed), F32),
            pltpu.VMEM((2, ROWS, packed), F32),
            pltpu.VMEM((ROWS, LANES), jnp.int32),
            pltpu.VMEM((near, ROWS, LANES), jnp.int32),
            pltpu.VMEM((3, ROWS, chunks * LANES), BF16),
            pltpu.VMEM((3, near, ROWS, chunks * LANES), BF16),
            pltpu.VMEM((ROWS, LANES), F32),
            pltpu.VMEM((cells * grps - 1, ROWS, LANES), F32),
            dma((4,)),
            dma((slots,)),
            dma((2, 3)),
            dma((2, 3)),
            dma((2,)),
            dma((2,)),
            dma((2,)),
            dma((3,)),
            dma((3,)),
            dma((2,)),
        ],
        compiler_params=pltpu.CompilerParams(collective_id=0, has_side_effects=True),
    )(initial_guess, right_side, camera_blocks, point_inverse, jacobian_tiles, tile_pattern.T, cell_load)
    return finish(first, second)


def solution(mesh):
    placed = (
        P(None, "cell"),
        P(None, "cell"),
        P(None, None, "cell"),
        P(None, None, ("cell", "grp")),
        P(("cell", "grp"), None, None),
        P(("cell", "grp"), None),
        P("cell"),
    )
    return jax.shard_map(
        functools.partial(per_device, mesh.shape["cell"], mesh.shape["grp"]),
        mesh=mesh,
        in_specs=placed,
        out_specs=(P(None, "cell"), P(None, "cell")),
        check_vma=False,
    )
```
